32 devices in a mesh: row: 8 (over z, x), col: 4 (over y, core).
Axes of the slice: x: 2, y: 2, z: 4, core: 2. Of those that a mesh axis runs over, the one named last changes fastest.
Arguments:
- training_input: float32 [256, 16384], P(None, 'row'), may hold values from -6 to 6
- query_cotangent: float32 [256, 16384], P(None, 'col'), may hold values from -6 to 6
- training_attention: float32 [256, 16384], P(None, 'col'), may hold values from -6 to 6
- output_cotangent: float32 [256, 16384], P(None, 'row'), may hold values from -6 to 6
- rollout_input: bfloat16 [512, 16384], P(None, 'row'), may hold values from -6 to 6
- query_weight: bfloat16 [16384, 16384], P('row', 'col'), may hold values from -0.046875 to 0.046875
- output_weight: bfloat16 [16384, 16384], P('col', 'row'), may hold values from -0.046875 to 0.046875
- cache_keys: bfloat16 [1024, 1024], P('row', 'col'), may hold values from -400 to 400
- cache_values: bfloat16 [1024, 1024], P('row', 'col'), may hold values from -96 to 96
- query_left: float32 [16384, 256], P('row', 'col'), may hold values from -6 to 6
- query_right: float32 [256, 16384], P('row', 'col'), may hold values from -6 to 6
- output_left: float32 [16384, 256], P('col', 'row'), may hold values from -6 to 6
- output_right: float32 [256, 16384], P('col', 'row'), may hold values from -6 to 6
- query_left_moment: float32 [16384, 256], P('row', 'col'), may hold values from -1.75 to 1.75
- query_left_square: float32 [16384, 256], P('row', 'col'), may hold values from 0.001 to 0.01
- query_right_moment: float32 [256, 16384], P('row', 'col'), may hold values from -1.75 to 1.75
- query_right_square: float32 [256, 16384], P('row', 'col'), may hold values from 0.001 to 0.01
- output_left_moment: float32 [16384, 256], P('col', 'row'), may hold values from -1.75 to 1.75
- output_left_square: float32 [16384, 256], P('col', 'row'), may hold values from 0.001 to 0.01
- output_right_moment: float32 [256, 16384], P('col', 'row'), may hold values from -1.75 to 1.75
- output_right_square: float32 [256, 16384], P('col', 'row'), may hold values from 0.001 to 0.01
Outputs:
- stepped_query_left: float32 [16384, 256], P('row', 'col')
- new_query_right: float32 [256, 16384], P('row', 'col')
- new_output_left: float32 [16384, 256], P('col', 'row')
- stepped_output_right: float32 [256, 16384], P('col', 'row')
- rollout_output: float32 [512, 16384], P('col', 'row')
The draws below stay inside these ranges and needn't reach their ends.
All inputs are finite; a program needn't handle non-finite values.
Results may differ from the reference program's by a relative error of at most 0.0055.
The reference program's roundings to bfloat16 on the way count: a program that leaves them out, or rounds other values in their place, can miss the bound.
Values may be sent and summed in bfloat16 or wider, within the bound.
A program may use at most 192 MiB of HBM per device.

```python
import math
import jax
import jax.numpy as jnp
from jax import lax

MODEL_WIDTH = 16384
HEAD_DIM = 128
KV_HEADS = 8
FACTOR_RANK = 256
PREFIX = 1024
TRAIN_ROWS = 256
ROLL_ROWS = 512
QUERY_WIDTH = 16384


def draw_cache_keys(key, part):
    width = KV_HEADS * HEAD_DIM
    base = jax.random.truncated_normal(key, -6.0, 6.0, (PREFIX, width), jnp.float32)
    return base.astype(jnp.bfloat16)


def steps_of(rng, shape, pieces, smallest, largest):
    factor_of, own = 1.0, jax.random.fold_in(rng, 6)
    for position, shards_of in pieces:
        draws = jnp.exp(jax.random.uniform(jax.random.fold_in(own, position), (shards_of,), jnp.float32, smallest / len(pieces), largest / len(pieces)))
        factor_of = factor_of * jnp.repeat(draws, shape[position] // shards_of).reshape([-1 if axis == position else 1 for axis in range(len(shape))])
    return factor_of


def centred(own_key, dims, spread, reach, shards=(), held_as=jnp.bfloat16):
    drawn = spread * jax.random.normal(own_key, dims, jnp.float32)
    if shards:
        drawn = drawn * steps_of(own_key, dims, shards, -0.22, 0.18)
    return jnp.clip(drawn, -reach, reach).astype(held_as)


def setup_inputs(seed: int = 0) -> dict:
    seeds = jax.random.split(jax.random.key(seed), 22)
    return {
        "training_input": centred(seeds[0], (TRAIN_ROWS, MODEL_WIDTH), 1.0, 6.0, ((1, 8),), jnp.float32),
        "query_cotangent": centred(seeds[1], (TRAIN_ROWS, QUERY_WIDTH), 1.0, 6.0, ((1, 4),), jnp.float32),
        "training_attention": centred(seeds[2], (TRAIN_ROWS, QUERY_WIDTH), 1.0, 6.0, ((1, 4),), jnp.float32),
        "output_cotangent": centred(seeds[3], (TRAIN_ROWS, MODEL_WIDTH), 1.0, 6.0, ((1, 8),), jnp.float32),
        "rollout_input": centred(seeds[4], (ROLL_ROWS, MODEL_WIDTH), 1.0, 6.0, ((1, 8),)),
        "query_weight": centred(seeds[5], (MODEL_WIDTH, QUERY_WIDTH), MODEL_WIDTH ** -0.5, 0.046875, ((0, 8), (1, 4))),
        "output_weight": centred(seeds[6], (QUERY_WIDTH, MODEL_WIDTH), QUERY_WIDTH ** -0.5, 0.046875, ((0, 4), (1, 8))),
        "cache_keys": draw_cache_keys(jax.random.fold_in(seeds[21], 71), 0),
        "cache_values": centred(seeds[8], (PREFIX, KV_HEADS * HEAD_DIM), 16.0, 96.0, ((0, 8), (1, 4))),
        "query_left": centred(seeds[9], (MODEL_WIDTH, FACTOR_RANK), 1.0, 6.0, ((0, 8), (1, 4)), jnp.float32),
        "query_right": centred(seeds[10], (FACTOR_RANK, QUERY_WIDTH), 1.0, 6.0, ((0, 8), (1, 4)), jnp.float32),
        "output_left": centred(seeds[11], (QUERY_WIDTH, FACTOR_RANK), 1.0, 6.0, ((0, 4), (1, 8)), jnp.float32),
        "output_right": centred(seeds[12], (FACTOR_RANK, MODEL_WIDTH), 1.0, 6.0, ((0, 4), (1, 8)), jnp.float32),
        "query_left_moment": centred(seeds[13], (MODEL_WIDTH, FACTOR_RANK), 0.3, 1.75, ((0, 8), (1, 4)), jnp.float32),
        "query_left_square": jnp.clip(jnp.exp(math.log(0.01) - 2.30258502 * jax.random.uniform(seeds[14], (MODEL_WIDTH, FACTOR_RANK), jnp.float32) ** steps_of(seeds[14], (MODEL_WIDTH, FACTOR_RANK), ((0, 8), (1, 4)), -0.2, 0.2)), 0.001, 0.01),
        "query_right_moment": centred(seeds[15], (FACTOR_RANK, QUERY_WIDTH), 0.3, 1.75, ((0, 8), (1, 4)), jnp.float32),
        "query_right_square": jnp.clip(jnp.exp(math.log(0.01) - 2.30258502 * jax.random.uniform(seeds[16], (FACTOR_RANK, QUERY_WIDTH), jnp.float32) ** steps_of(seeds[16], (FACTOR_RANK, QUERY_WIDTH), ((0, 8), (1, 4)), -0.2, 0.2)), 0.001, 0.01),
        "output_left_moment": centred(seeds[17], (QUERY_WIDTH, FACTOR_RANK), 0.3, 1.75, ((0, 4), (1, 8)), jnp.float32),
        "output_left_square": jnp.clip(jnp.exp(math.log(0.01) - 2.30258502 * jax.random.uniform(seeds[18], (QUERY_WIDTH, FACTOR_RANK), jnp.float32) ** steps_of(seeds[18], (QUERY_WIDTH, FACTOR_RANK), ((0, 4), (1, 8)), -0.2, 0.2)), 0.001, 0.01),
        "output_right_moment": centred(seeds[19], (FACTOR_RANK, MODEL_WIDTH), 0.3, 1.75, ((0, 4), (1, 8)), jnp.float32),
        "output_right_square": jnp.clip(jnp.exp(math.log(0.01) - 2.30258502 * jax.random.uniform(seeds[20], (FACTOR_RANK, MODEL_WIDTH), jnp.float32) ** steps_of(seeds[20], (FACTOR_RANK, MODEL_WIDTH), ((0, 4), (1, 8)), -0.2, 0.2)), 0.001, 0.01),
    }


highest = lax.Precision.HIGHEST
learn_rate = 0.03
beta_first = 0.9
beta_second = 0.999
epsilon = 1e-08
weight_decay = 0.1
first_corr = 1.0 - 0.9 ** 50 * 0.9 ** 50
second_corr = 1.0 - 0.999 ** 50 * 0.999 ** 50

def exact_matrix_product(left, right):
    return jnp.dot(left, right, precision=highest, preferred_element_type=jnp.float32)

def adamw_update(factor, gradient, moment, square):
    moment = beta_first * moment + (1.0 - beta_first) * gradient
    square = beta_second * square + (1.0 - beta_second) * gradient * gradient
    change = moment / first_corr / (jnp.sqrt(square / second_corr) + epsilon) + weight_decay * factor
    return factor - learn_rate * change

def attend(query_rows, keys_all, values_all, heads_local):
    total_rows = query_rows.shape[0]
    head_dim = keys_all.shape[1] // heads_local
    group_size = query_rows.shape[1] // keys_all.shape[1]
    row_block = math.gcd(total_rows, 128)
    grouped = query_rows.reshape(total_rows // row_block, row_block, heads_local, group_size, head_dim)
    keys_three = keys_all.reshape(keys_all.shape[0], heads_local, head_dim).astype(jnp.float32)
    values_three = values_all.reshape(values_all.shape[0], heads_local, head_dim).astype(jnp.float32)

    def one_block(queries):
        scores = jnp.einsum('bkgd,ckd->bkgc', queries.astype(jnp.float32), keys_three, precision=highest) * head_dim ** (-0.5)
        highest_score = lax.optimization_barrier(jnp.max(scores, axis=-1, keepdims=True))
        exponent = jnp.exp(scores - highest_score)
        weights = (exponent / lax.optimization_barrier(jnp.sum(exponent, axis=-1, keepdims=True))).astype(jnp.bfloat16)
        mixture = jnp.einsum('bkgc,ckd->bkgd', weights.astype(jnp.float32), values_three, precision=highest)
        return mixture.astype(jnp.bfloat16)
    blocks = lax.map(one_block, grouped)
    return blocks.reshape(total_rows, heads_local * group_size * head_dim)

def reference(training_input, query_cotangent, training_attention, output_cotangent, rollout_input, query_weight, output_weight, cache_keys, cache_values, query_left, query_right, output_left, output_right, query_left_moment, query_left_square, query_right_moment, query_right_square, output_left_moment, output_left_square, output_right_moment, output_right_square):
    adapter_scale = 1.0 / math.sqrt(MODEL_WIDTH * FACTOR_RANK)
    cotangent_product = exact_matrix_product(query_cotangent, query_right.T)
    attention_product = exact_matrix_product(training_attention, output_left)
    input_product = exact_matrix_product(training_input, query_left)
    output_cotangent_product = exact_matrix_product(output_cotangent, output_right.T)
    query_left_gradient = adapter_scale * exact_matrix_product(training_input.T, cotangent_product)
    query_right_gradient = adapter_scale * exact_matrix_product(input_product.T, query_cotangent)
    output_left_gradient = adapter_scale * exact_matrix_product(training_attention.T, output_cotangent_product)
    output_right_gradient = adapter_scale * exact_matrix_product(attention_product.T, output_cotangent)
    stepped_query_left = adamw_update(query_left, query_left_gradient, query_left_moment, query_left_square)
    new_query_right = adamw_update(query_right, query_right_gradient, query_right_moment, query_right_square)
    new_output_left = adamw_update(output_left, output_left_gradient, output_left_moment, output_left_square)
    stepped_output_right = adamw_update(output_right, output_right_gradient, output_right_moment, output_right_square)
    group_cols = QUERY_WIDTH // KV_HEADS
    indices = jnp.arange(KV_HEADS, dtype=jnp.int32)

    def query_group(index):
        offset = index * group_cols
        weight_column_count = lax.dynamic_slice_in_dim(query_weight, offset, group_cols, 1)
        right_column_block = lax.dynamic_slice_in_dim(new_query_right, offset, group_cols, 1)
        merged_weight_pair = (weight_column_count.astype(jnp.float32) + adapter_scale * exact_matrix_product(stepped_query_left, right_column_block)).astype(jnp.bfloat16)
        return jnp.dot(rollout_input, merged_weight_pair, preferred_element_type=jnp.float32).astype(jnp.bfloat16)
    query_parts = lax.map(query_group, indices)
    rollout_query = jnp.transpose(query_parts, (1, 0, 2)).reshape(ROLL_ROWS, QUERY_WIDTH)
    attended = attend(rollout_query, cache_keys, cache_values, KV_HEADS)

    def output_group(running, index):
        offset = index * group_cols
        weight_row_count = lax.dynamic_slice_in_dim(output_weight, offset, group_cols, 0)
        left_row_block = lax.dynamic_slice_in_dim(new_output_left, offset, group_cols, 0)
        merged_weight_pair = (weight_row_count.astype(jnp.float32) + adapter_scale * exact_matrix_product(left_row_block, stepped_output_right)).astype(jnp.bfloat16)
        portion = lax.dynamic_slice_in_dim(attended, offset, group_cols, 1)
        return (running + jnp.dot(portion, merged_weight_pair, preferred_element_type=jnp.float32), None)
    rollout_output, unused = lax.scan(output_group, jnp.zeros((ROLL_ROWS, MODEL_WIDTH), jnp.float32), indices)
    return (stepped_query_left, new_query_right, new_output_left, stepped_output_right, rollout_output)
```

```python
import functools
import math

import jax
import jax.numpy as jnp
from jax import lax
from jax.experimental import pallas as pl
from jax.experimental.pallas import tpu as pltpu
from jax.sharding import PartitionSpec as P

MODEL_WIDTH = 16384
HEAD_DIM = 128
FACTOR_RANK = 256


high = lax.Precision.HIGH
learn_rate = 0.03
beta_first = 0.9
beta_second = 0.999
epsilon = 1e-08
weight_decay = 0.1
first_corr = 1.0 - 0.9**50 * 0.9**50
second_corr = 1.0 - 0.999**50 * 0.999**50


def high_product(left, right):
    return jnp.dot(left, right, precision=high, preferred_element_type=jnp.float32)


def turned_product(left, right):
    return lax.dot_general(
        left,
        right,
        (((1,), (1,)), ((), ())),
        precision=high,
        preferred_element_type=jnp.float32,
    )


def adamw_update(factor, gradient, moment, square):
    moment = beta_first * moment + (1.0 - beta_first) * gradient
    square = beta_second * square + (1.0 - beta_second) * gradient * gradient
    change = (
        moment / first_corr / (jnp.sqrt(square / second_corr) + epsilon) + weight_decay * factor
    )
    return factor - learn_rate * change


def split_pair(value):
    upper = value.astype(jnp.bfloat16)
    return upper, (value - upper.astype(jnp.float32)).astype(jnp.bfloat16)


def merged_block(left_upper, left_lower, right_value, weight, scale):
    right_upper, right_lower = split_pair(right_value)
    delta = jnp.dot(left_upper, right_upper, preferred_element_type=jnp.float32)
    delta += jnp.dot(left_upper, right_lower, preferred_element_type=jnp.float32)
    delta += jnp.dot(left_lower, right_upper, preferred_element_type=jnp.float32)
    return (weight.astype(jnp.float32) + scale * delta).astype(jnp.bfloat16)


def keep_left(left_ref, upper_ref, lower_ref, block):
    @pl.when(pl.program_id(0) == 0)
    def _():
        upper, lower = split_pair(left_ref[...].T)
        upper_ref[block] = upper
        lower_ref[block] = lower


def project_kernel(scale, x_ref, left_ref, right_ref, weight_ref, out_ref, upper_ref, lower_ref):
    block = pl.program_id(1)
    keep_left(left_ref, upper_ref, lower_ref, block)
    merged = merged_block(
        upper_ref[block], lower_ref[block], right_ref[...], weight_ref[...], scale
    )
    part = jnp.dot(x_ref[...], merged, preferred_element_type=jnp.float32)

    @pl.when(block == 0)
    def _():
        out_ref[...] = part

    @pl.when(block > 0)
    def _():
        out_ref[...] += part


def merge_kernel(scale, left_ref, right_ref, weight_ref, out_ref, upper_ref, lower_ref):
    block = pl.program_id(1)
    keep_left(left_ref, upper_ref, lower_ref, block)
    out_ref[...] = merged_block(
        upper_ref[block], lower_ref[block], right_ref[...], weight_ref[...], scale
    )


def left_scratch(blocks, tile, rank):
    return [
        pltpu.VMEM((blocks, tile, rank), jnp.bfloat16),
        pltpu.VMEM((blocks, tile, rank), jnp.bfloat16),
    ]


def project_merged(scale, x, left_turned, right, weight, start, width):
    depth = weight.shape[0]
    rank = right.shape[0]
    rows = x.shape[0]
    tile_depth, tile_width = math.gcd(depth, 512), math.gcd(width, 512)
    blocks = depth // tile_depth
    first = start // tile_width
    return pl.pallas_call(
        functools.partial(project_kernel, scale),
        grid=(width // tile_width, blocks),
        in_specs=[
            pl.BlockSpec((rows, tile_depth), lambda j, k: (0, k)),
            pl.BlockSpec((rank, tile_depth), lambda j, k: (0, jnp.where(j == 0, k, blocks - 1))),
            pl.BlockSpec((rank, tile_width), lambda j, k: (0, first + j)),
            pl.BlockSpec((tile_depth, tile_width), lambda j, k: (k, first + j)),
        ],
        out_specs=pl.BlockSpec((rows, tile_width), lambda j, k: (0, j)),
        out_shape=jax.ShapeDtypeStruct((rows, width), jnp.float32),
        scratch_shapes=left_scratch(blocks, tile_depth, rank),
        compiler_params=pltpu.CompilerParams(
            dimension_semantics=("arbitrary", "arbitrary"), vmem_limit_bytes=32 * 2**20
        ),
        cost_estimate=pl.CostEstimate(
            flops=2 * depth * width * (3 * rank + rows),
            bytes_accessed=2 * depth * width + 4 * rows * width,
            transcendentals=0,
        ),
    )(x, left_turned, right, weight)


def merge_weight(scale, left_turned, right, weight):
    depth, width = weight.shape
    rank = right.shape[0]
    tile_depth, tile_width = math.gcd(depth, 512), math.gcd(width, 512)
    blocks = depth // tile_depth
    return pl.pallas_call(
        functools.partial(merge_kernel, scale),
        grid=(width // tile_width, blocks),
        in_specs=[
            pl.BlockSpec((rank, tile_depth), lambda j, k: (0, jnp.where(j == 0, k, blocks - 1))),
            pl.BlockSpec((rank, tile_width), lambda j, k: (0, j)),
            pl.BlockSpec((tile_depth, tile_width), lambda j, k: (k, j)),
        ],
        out_specs=pl.BlockSpec((tile_depth, tile_width), lambda j, k: (k, j)),
        out_shape=jax.ShapeDtypeStruct((depth, width), jnp.bfloat16),
        scratch_shapes=left_scratch(blocks, tile_depth, rank),
        compiler_params=pltpu.CompilerParams(
            dimension_semantics=("arbitrary", "arbitrary"), vmem_limit_bytes=32 * 2**20
        ),
        cost_estimate=pl.CostEstimate(
            flops=6 * depth * width * rank,
            bytes_accessed=4 * depth * width,
            transcendentals=0,
        ),
    )(left_turned, right, weight)


def attend_kernel(head_dim, q_ref, k_ref, v_ref, out_ref):
    rows, width = q_ref.shape
    heads = width // head_dim
    queries = jnp.concatenate(
        [q_ref[:, h * head_dim : (h + 1) * head_dim] for h in range(heads)], axis=0
    ).astype(jnp.bfloat16)
    scores = lax.dot_general(
        queries, k_ref[...], (((1,), (1,)), ((), ())), preferred_element_type=jnp.float32
    ) * head_dim ** (-0.5)
    exponent = jnp.exp(scores - jnp.max(scores, axis=-1, keepdims=True))
    weights = (exponent / jnp.sum(exponent, axis=-1, keepdims=True)).astype(jnp.bfloat16)
    mixture = jnp.dot(weights, v_ref[...], preferred_element_type=jnp.float32)
    mixture = mixture.astype(jnp.bfloat16)
    for h in range(heads):
        out_ref[:, h * head_dim : (h + 1) * head_dim] = mixture[h * rows : (h + 1) * rows]


def attend(query_rows, keys, values, head, key_heads):
    rows, width = query_rows.shape
    positions = keys.shape[0]
    head_dim = HEAD_DIM
    tile = head_dim * math.gcd(width // head_dim, max(1, 512 // rows))
    return pl.pallas_call(
        functools.partial(attend_kernel, head_dim),
        grid=(width // tile,),
        in_specs=[
            pl.BlockSpec((rows, tile), lambda i: (0, i)),
            pl.BlockSpec((positions, head_dim), lambda i: (0, head)),
            pl.BlockSpec((positions, head_dim), lambda i: (0, key_heads + head)),
        ],
        out_specs=pl.BlockSpec((rows, tile), lambda i: (0, i)),
        out_shape=jax.ShapeDtypeStruct((rows, width), jnp.bfloat16),
        compiler_params=pltpu.CompilerParams(
            dimension_semantics=("arbitrary",), vmem_limit_bytes=32 * 2**20
        ),
        cost_estimate=pl.CostEstimate(
            flops=4 * rows * width * positions,
            bytes_accessed=6 * rows * width + 4 * positions * head_dim,
            transcendentals=rows * width // head_dim * positions,
        ),
    )(query_rows, keys, values)


def local(
    training_input,
    query_cotangent,
    training_attention,
    output_cotangent,
    rollout_input,
    query_weight,
    output_weight,
    cache_keys,
    cache_values,
    query_left,
    query_right,
    output_left,
    output_right,
    query_left_moment,
    query_left_square,
    query_right_moment,
    query_right_square,
    output_left_moment,
    output_left_square,
    output_right_moment,
    output_right_square,
):
    adapter_scale = 1.0 / math.sqrt(MODEL_WIDTH * FACTOR_RANK)
    input_turned = turned_product(query_left.T, training_input)
    outcot_turned = turned_product(output_right, output_cotangent)
    input_every = lax.all_gather(
        jnp.concatenate((input_turned, outcot_turned), axis=1), "col", axis=0, tiled=True
    )
    input_rank = lax.psum_scatter(input_every, "row", scatter_dimension=0, tiled=True)
    cotan_turned = turned_product(query_right, query_cotangent)
    attn_turned = turned_product(output_left.T, training_attention)
    cotan_every = lax.all_gather(
        jnp.concatenate((cotan_turned, attn_turned), axis=1), "row", axis=0, tiled=True
    )
    cotan_rank = lax.psum_scatter(cotan_every, "col", scatter_dimension=0, tiled=True)
    rows = training_input.shape[0]
    query_left_gradient = adapter_scale * high_product(cotan_rank[:, :rows], training_input).T
    query_right_gradient = adapter_scale * high_product(input_rank[:, :rows], query_cotangent)
    output_left_gradient = adapter_scale * high_product(input_rank[:, rows:], training_attention).T
    output_right_gradient = adapter_scale * high_product(cotan_rank[:, rows:], output_cotangent)
    new_query_right = adamw_update(
        query_right, query_right_gradient, query_right_moment, query_right_square
    )
    stepped_query_left = adamw_update(
        query_left, query_left_gradient, query_left_moment, query_left_square
    )
    new_output_left = adamw_update(
        output_left, output_left_gradient, output_left_moment, output_left_square
    )
    stepped_output_right = adamw_update(
        output_right, output_right_gradient, output_right_moment, output_right_square
    )
    next_query_right = lax.all_gather(new_query_right, "row", axis=0, tiled=True)
    next_query_left = lax.all_gather(stepped_query_left.T, "col", axis=0, tiled=True)
    next_output_left = lax.all_gather(new_output_left.T, "row", axis=0, tiled=True)
    next_output_right = lax.all_gather(stepped_output_right, "col", axis=0, tiled=True)
    cache_all = lax.all_gather(
        jnp.concatenate((cache_keys, cache_values), axis=1), "row", axis=0, tiled=True
    )
    key_heads = cache_keys.shape[1] // HEAD_DIM
    width = query_weight.shape[1] // key_heads
    queries = [
        lax.psum_scatter(
            project_merged(
                adapter_scale,
                rollout_input,
                next_query_left,
                next_query_right,
                query_weight,
                head * width,
                width,
            ),
            "row",
            scatter_dimension=0,
            tiled=True,
        )
        for head in range(key_heads)
    ]
    merged_output = merge_weight(
        adapter_scale, next_output_left, next_output_right, output_weight
    )
    attended = [
        lax.all_gather(
            attend(queries[head], cache_all, cache_all, head, key_heads),
            "row",
            axis=0,
            tiled=True,
        )
        for head in range(key_heads)
    ]
    portion = sum(
        jnp.dot(
            attended[head],
            merged_output[head * width : (head + 1) * width],
            preferred_element_type=jnp.float32,
        )
        for head in range(key_heads)
    )
    rollout_output = lax.psum_scatter(portion, "col", scatter_dimension=0, tiled=True)
    return (
        stepped_query_left,
        new_query_right,
        new_output_left,
        stepped_output_right,
        rollout_output,
    )


def solution(mesh):
    placed = (
        P(None, "row"),
        P(None, "col"),
        P(None, "col"),
        P(None, "row"),
        P(None, "row"),
        P("row", "col"),
        P("col", "row"),
        P("row", "col"),
        P("row", "col"),
        P("row", "col"),
        P("row", "col"),
        P("col", "row"),
        P("col", "row"),
        P("row", "col"),
        P("row", "col"),
        P("row", "col"),
        P("row", "col"),
        P("col", "row"),
        P("col", "row"),
        P("col", "row"),
        P("col", "row"),
    )
    return jax.shard_map(
        local,
        mesh=mesh,
        in_specs=placed,
        out_specs=(
            P("row", "col"),
            P("row", "col"),
            P("col", "row"),
            P("col", "row"),
            P("col", "row"),
        ),
        check_vma=False,
    )
```

```python
import functools
import math

import jax
import jax.numpy as jnp
from jax import lax
from jax.experimental import pallas as pl
from jax.experimental.pallas import tpu as pltpu
from jax.sharding import PartitionSpec as P

MODEL_WIDTH = 16384
HEAD_DIM = 128
FACTOR_RANK = 256


high = lax.Precision.HIGH
learn_rate = 0.03
beta_first = 0.9
beta_second = 0.999
epsilon = 1e-08
weight_decay = 0.1
first_corr = 1.0 - 0.9**50 * 0.9**50
second_corr = 1.0 - 0.999**50 * 0.999**50


def high_product(left, right):
    return jnp.dot(left, right, precision=high, preferred_element_type=jnp.float32)


def turned_product(left, right):
    return lax.dot_general(
        left,
        right,
        (((1,), (1,)), ((), ())),
        precision=high,
        preferred_element_type=jnp.float32,
    )


def adamw_update(factor, gradient, moment, square):
    moment = beta_first * moment + (1.0 - beta_first) * gradient
    square = beta_second * square + (1.0 - beta_second) * gradient * gradient
    change = (
        moment / first_corr / (jnp.sqrt(square / second_corr) + epsilon) + weight_decay * factor
    )
    return factor - learn_rate * change


def split_pair(value):
    upper = value.astype(jnp.bfloat16)
    return upper, (value - upper.astype(jnp.float32)).astype(jnp.bfloat16)


def merged_block(left_upper, left_lower, right_value, weight, scale):
    right_upper, right_lower = split_pair(right_value)
    delta = jnp.dot(left_upper, right_upper, preferred_element_type=jnp.float32)
    delta += jnp.dot(left_upper, right_lower, preferred_element_type=jnp.float32)
    delta += jnp.dot(left_lower, right_upper, preferred_element_type=jnp.float32)
    return (weight.astype(jnp.float32) + scale * delta).astype(jnp.bfloat16)


def keep_left(left_ref, upper_ref, lower_ref, block):
    @pl.when(pl.program_id(0) == 0)
    def _():
        upper, lower = split_pair(left_ref[...].T)
        upper_ref[block] = upper
        lower_ref[block] = lower


def project_kernel(scale, x_ref, left_ref, right_ref, weight_ref, out_ref, upper_ref, lower_ref):
    block = pl.program_id(1)
    keep_left(left_ref, upper_ref, lower_ref, block)
    merged = merged_block(
        upper_ref[block], lower_ref[block], right_ref[...], weight_ref[...], scale
    )
    part = jnp.dot(x_ref[...], merged, preferred_element_type=jnp.float32)

    @pl.when(block == 0)
    def _():
        out_ref[...] = part

    @pl.when(block > 0)
    def _():
        out_ref[...] += part


def merge_kernel(scale, left_ref, right_ref, weight_ref, out_ref, upper_ref, lower_ref):
    block = pl.program_id(1)
    keep_left(left_ref, upper_ref, lower_ref, block)
    out_ref[...] = merged_block(
        upper_ref[block], lower_ref[block], right_ref[...], weight_ref[...], scale
    )


def left_scratch(blocks, tile, rank):
    return [
        pltpu.VMEM((blocks, tile, rank), jnp.bfloat16),
        pltpu.VMEM((blocks, tile, rank), jnp.bfloat16),
    ]


def project_merged(scale, x, left_turned, right, weight, start, width):
    depth = weight.shape[0]
    rank = right.shape[0]
    rows = x.shape[0]
    tile_depth, tile_width = math.gcd(depth, 512), math.gcd(width, 512)
    blocks = depth // tile_depth
    first = start // tile_width
    return pl.pallas_call(
        functools.partial(project_kernel, scale),
        grid=(width // tile_width, blocks),
        in_specs=[
            pl.BlockSpec((rows, tile_depth), lambda j, k: (0, k)),
            pl.BlockSpec((rank, tile_depth), lambda j, k: (0, jnp.where(j == 0, k, blocks - 1))),
            pl.BlockSpec((rank, tile_width), lambda j, k: (0, first + j)),
            pl.BlockSpec((tile_depth, tile_width), lambda j, k: (k, first + j)),
        ],
        out_specs=pl.BlockSpec((rows, tile_width), lambda j, k: (0, j)),
        out_shape=jax.ShapeDtypeStruct((rows, width), jnp.float32),
        scratch_shapes=left_scratch(blocks, tile_depth, rank),
        compiler_params=pltpu.CompilerParams(
            dimension_semantics=("arbitrary", "arbitrary"), vmem_limit_bytes=32 * 2**20
        ),
        cost_estimate=pl.CostEstimate(
            flops=2 * depth * width * (3 * rank + rows),
            bytes_accessed=2 * depth * width + 4 * rows * width,
            transcendentals=0,
        ),
    )(x, left_turned, right, weight)


def merge_weight(scale, left_turned, right, weight):
    depth, width = weight.shape
    rank = right.shape[0]
    tile_depth, tile_width = math.gcd(depth, 512), math.gcd(width, 512)
    blocks = depth // tile_depth
    return pl.pallas_call(
        functools.partial(merge_kernel, scale),
        grid=(width // tile_width, blocks),
        in_specs=[
            pl.BlockSpec((rank, tile_depth), lambda j, k: (0, jnp.where(j == 0, k, blocks - 1))),
            pl.BlockSpec((rank, tile_width), lambda j, k: (0, j)),
            pl.BlockSpec((tile_depth, tile_width), lambda j, k: (k, j)),
        ],
        out_specs=pl.BlockSpec((tile_depth, tile_width), lambda j, k: (k, j)),
        out_shape=jax.ShapeDtypeStruct((depth, width), jnp.bfloat16),
        scratch_shapes=left_scratch(blocks, tile_depth, rank),
        compiler_params=pltpu.CompilerParams(
            dimension_semantics=("arbitrary", "arbitrary"), vmem_limit_bytes=32 * 2**20
        ),
        cost_estimate=pl.CostEstimate(
            flops=6 * depth * width * rank,
            bytes_accessed=4 * depth * width,
            transcendentals=0,
        ),
    )(left_turned, right, weight)


def attend_kernel(head_dim, q_ref, k_ref, v_ref, out_ref):
    rows, width = q_ref.shape
    heads = width // head_dim
    queries = jnp.concatenate(
        [q_ref[:, h * head_dim : (h + 1) * head_dim] for h in range(heads)], axis=0
    ).astype(jnp.bfloat16)
    scores = lax.dot_general(
        queries, k_ref[...], (((1,), (1,)), ((), ())), preferred_element_type=jnp.float32
    ) * head_dim ** (-0.5)
    exponent = jnp.exp(scores - jnp.max(scores, axis=-1, keepdims=True))
    weights = (exponent / jnp.sum(exponent, axis=-1, keepdims=True)).astype(jnp.bfloat16)
    mixture = jnp.dot(weights, v_ref[...], preferred_element_type=jnp.float32)
    mixture = mixture.astype(jnp.bfloat16)
    for h in range(heads):
        out_ref[:, h * head_dim : (h + 1) * head_dim] = mixture[h * rows : (h + 1) * rows]


def attend(query_rows, keys, values, head, key_heads):
    rows, width = query_rows.shape
    positions = keys.shape[0]
    head_dim = HEAD_DIM
    tile = head_dim * math.gcd(width // head_dim, max(1, 512 // rows))
    return pl.pallas_call(
        functools.partial(attend_kernel, head_dim),
        grid=(width // tile,),
        in_specs=[
            pl.BlockSpec((rows, tile), lambda i: (0, i)),
            pl.BlockSpec((positions, head_dim), lambda i: (0, head)),
            pl.BlockSpec((positions, head_dim), lambda i: (0, key_heads + head)),
        ],
        out_specs=pl.BlockSpec((rows, tile), lambda i: (0, i)),
        out_shape=jax.ShapeDtypeStruct((rows, width), jnp.bfloat16),
        compiler_params=pltpu.CompilerParams(
            dimension_semantics=("arbitrary",), vmem_limit_bytes=32 * 2**20
        ),
        cost_estimate=pl.CostEstimate(
            flops=4 * rows * width * positions,
            bytes_accessed=6 * rows * width + 4 * positions * head_dim,
            transcendentals=rows * width // head_dim * positions,
        ),
    )(query_rows, keys, values)


def exchange_sum(value, axis):
    count = lax.axis_size(axis)
    blocks = value.reshape(count, value.shape[0] // count, value.shape[1])
    received = lax.all_to_all(blocks, axis, 0, 0)
    return jnp.sum(received.astype(jnp.float32), axis=0)


def scatter_sum(value, axis):
    return lax.psum_scatter(value, axis, scatter_dimension=0, tiled=True)


def local(
    training_input,
    query_cotangent,
    training_attention,
    output_cotangent,
    rollout_input,
    query_weight,
    output_weight,
    cache_keys,
    cache_values,
    query_left,
    query_right,
    output_left,
    output_right,
    query_left_moment,
    query_left_square,
    query_right_moment,
    query_right_square,
    output_left_moment,
    output_left_square,
    output_right_moment,
    output_right_square,
):
    adapter_scale = 1.0 / math.sqrt(MODEL_WIDTH * FACTOR_RANK)
    input_turned = turned_product(query_left.T, training_input)
    outcot_turned = turned_product(output_right, output_cotangent)
    input_every = lax.all_gather(
        jnp.concatenate((input_turned, outcot_turned), axis=1), "col", axis=0, tiled=True
    )
    input_rank = exchange_sum(input_every, "row")
    cotan_turned = turned_product(query_right, query_cotangent)
    attn_turned = turned_product(output_left.T, training_attention)
    cotan_every = lax.all_gather(
        jnp.concatenate((cotan_turned, attn_turned), axis=1), "row", axis=0, tiled=True
    )
    cotan_rank = exchange_sum(cotan_every, "col")
    rows = training_input.shape[0]
    query_left_gradient = adapter_scale * high_product(cotan_rank[:, :rows], training_input).T
    query_right_gradient = adapter_scale * high_product(input_rank[:, :rows], query_cotangent)
    output_left_gradient = adapter_scale * high_product(input_rank[:, rows:], training_attention).T
    output_right_gradient = adapter_scale * high_product(cotan_rank[:, rows:], output_cotangent)
    new_query_right = adamw_update(
        query_right, query_right_gradient, query_right_moment, query_right_square
    )
    stepped_query_left = adamw_update(
        query_left, query_left_gradient, query_left_moment, query_left_square
    )
    new_output_left = adamw_update(
        output_left, output_left_gradient, output_left_moment, output_left_square
    )
    stepped_output_right = adamw_update(
        output_right, output_right_gradient, output_right_moment, output_right_square
    )
    next_query_right = lax.all_gather(new_query_right, "row", axis=0, tiled=True)
    next_query_left = lax.all_gather(stepped_query_left.T, "col", axis=0, tiled=True)
    next_output_left = lax.all_gather(new_output_left.T, "row", axis=0, tiled=True)
    next_output_right = lax.all_gather(stepped_output_right, "col", axis=0, tiled=True)
    cache_all = lax.all_gather(
        jnp.concatenate((cache_keys, cache_values), axis=1), "row", axis=0, tiled=True
    )
    key_heads = cache_keys.shape[1] // HEAD_DIM
    width = query_weight.shape[1] // key_heads
    queries = [
        (exchange_sum if head % 2 else scatter_sum)(
            project_merged(
                adapter_scale,
                rollout_input,
                next_query_left,
                next_query_right,
                query_weight,
                head * width,
                width,
            ),
            "row",
        )
        for head in range(key_heads)
    ]
    merged_output = merge_weight(
        adapter_scale, next_output_left, next_output_right, output_weight
    )
    attended = [
        lax.all_gather(
            attend(queries[head], cache_all, cache_all, head, key_heads),
            "row",
            axis=0,
            tiled=True,
        )
        for head in range(key_heads)
    ]
    portion = sum(
        jnp.dot(
            attended[head],
            merged_output[head * width : (head + 1) * width],
            preferred_element_type=jnp.float32,
        )
        for head in range(key_heads)
    )
    rollout_output = exchange_sum(portion.astype(jnp.bfloat16), "col")
    return (
        stepped_query_left,
        new_query_right,
        new_output_left,
        stepped_output_right,
        rollout_output,
    )


def solution(mesh):
    placed = (
        P(None, "row"),
        P(None, "col"),
        P(None, "col"),
        P(None, "row"),
        P(None, "row"),
        P("row", "col"),
        P("col", "row"),
        P("row", "col"),
        P("row", "col"),
        P("row", "col"),
        P("row", "col"),
        P("col", "row"),
        P("col", "row"),
        P("row", "col"),
        P("row", "col"),
        P("row", "col"),
        P("row", "col"),
        P("col", "row"),
        P("col", "row"),
        P("col", "row"),
        P("col", "row"),
    )
    return jax.shard_map(
        local,
        mesh=mesh,
        in_specs=placed,
        out_specs=(
            P("row", "col"),
            P("row", "col"),
            P("col", "row"),
            P("col", "row"),
            P("col", "row"),
        ),
        check_vma=False,
    )
```
